256 devices in a mesh: dp: 8 (over y, core), expert: 32 (over z, x).
Axes of the slice: x: 4, y: 4, z: 8, core: 2. Of those that a mesh axis runs over, the one named last changes fastest.
Arguments:
- tokens: bfloat16 [32768, 4096], P(('dp', 'expert')), may hold values from -6 to 6
- out_grad: bfloat16 [32768, 4096], P(('dp', 'expert')), may hold values from -0.29882812 to 0.29882812
- probs: bfloat16 [32768, 8], P(('dp', 'expert')), may hold values from 0.049804688 to 0.5
- routes: int32 [32768, 8], P(('dp', 'expert')), may hold values from 0 to 127, as said below
- saved_gate: bfloat16 [131072, 768], P(('dp', 'expert')), may hold values from -6 to 6
- saved_up: bfloat16 [131072, 768], P(('dp', 'expert')), may hold values from -6 to 6
- down_weight: bfloat16 [32, 768, 4096], P('expert'), may hold values from -0.21875 to 0.21875
Outputs:
- grad_down: float32 [32, 768, 4096], P('expert', 'dp')
- grad_up: bfloat16 [32, 4096, 768], P('expert', 'dp')
- prob_grad: float32 [32768, 8], P(('dp', 'expert'))
The draws below stay inside these ranges and needn't reach their ends.
Inputs may be any that keep to these rules, and one draw needn't show every extreme that they name: `routes`: each row names 8 different experts. In every aligned block of 128 rows at least half of the rows name one common expert whose number is a multiple of 4; which one is drawn from the seed.
All inputs are finite; a program needn't handle non-finite values.
Results may differ from the reference program's by a relative error of at most 0.014.
Values may be sent and summed in bfloat16 or wider, within the bound.
A program may use at most 192 MiB of HBM per device.

```python
import jax
import jax.numpy as jnp
from jax import lax

D = 4096
FF = 768
TOP = 8
EXP_DEV = 4
TOK_DEV = 128
EXPERTS = 128
WINDOW = 32
CAP = 16
TOKENS = 32768
SLOTS = 131072
N_DP = 8


def draw_routes(key, part):
    base_key, bias_key, hot_key, parity_key = jax.random.split(jax.random.fold_in(key, 17), 4)
    base_score = jax.random.randint(base_key, (TOKENS, EXPERTS), 0, 1 << 20)
    bias_score = jax.random.randint(bias_key, (EXPERTS,), 0, 3) * (1 << 19)
    windows = EXPERTS // EXP_DEV
    hot_expert = jax.random.randint(hot_key, (), 0, windows) * EXP_DEV
    parity = jax.random.randint(parity_key, (), 0, 2)
    row_ids = jnp.arange(TOKENS, dtype=jnp.int32)
    column_ids = jnp.arange(EXPERTS, dtype=jnp.int32)
    lifted = ((row_ids + parity) % 2 == 0)[:, None] & (column_ids == hot_expert)[None, :]
    scores = base_score + bias_score[None, :] + jnp.where(lifted, 1 << 21, 0)
    scores = scores * EXPERTS + column_ids[None, :]
    picked = lax.top_k(scores, TOP)[1]
    return picked.astype(jnp.int32)


def block_levels(own_key, dims, cuts, smallest, largest):
    loudness = 1.0
    for dim, parts in cuts:
        heights = jax.random.uniform(jax.random.fold_in(jax.random.fold_in(own_key, 6), dim), (parts,), jnp.float32, smallest / len(cuts), largest / len(cuts))
        loudness = loudness * jnp.repeat(jnp.exp(heights), dims[dim] // parts).reshape((-1,) + (1,) * (len(dims) - 1 - dim))
    return loudness


def noise(own_key, shape, spread, most, cuts=(), kind=jnp.bfloat16):
    array = spread * jax.random.normal(own_key, shape, jnp.float32)
    if cuts:
        array = array * block_levels(own_key, shape, cuts, -0.22, 0.18)
    return jnp.clip(array, -most, most).astype(kind)


def setup_inputs(seed: int = 0) -> dict:
    streams_of = jax.random.split(jax.random.key(seed), 8)
    tokens = noise(streams_of[0], (TOKENS, D), 1.0, 6.0, ((0, 256),))
    out_grad = noise(streams_of[1], (TOKENS, D), 0.05, 0.29882812, ((0, 256),))
    probs = jnp.clip(0.049804688 + 0.4501953 * jax.random.uniform(streams_of[2], (TOKENS, TOP), jnp.float32) ** block_levels(streams_of[2], (TOKENS, TOP), ((0, 256),), -0.2, 0.2), 0.049804688, 0.5).astype(jnp.bfloat16)
    routes = draw_routes(jax.random.fold_in(streams_of[7], 71), 0)
    saved_gate = noise(streams_of[4], (SLOTS, FF), 1.0, 6.0, ((0, 256),))
    saved_up = noise(streams_of[5], (SLOTS, FF), 1.0, 6.0, ((0, 256),))
    down_weight = noise(streams_of[6], (WINDOW, FF, D), FF ** -0.5, 0.21875, ((0, 32),))
    return {"tokens": tokens, "out_grad": out_grad, "probs": probs, "routes": routes, "saved_gate": saved_gate, "saved_up": saved_up, "down_weight": down_weight}


def reference(tokens, out_grad, probs, routes, saved_gate, saved_up, down_weight):
    owners = EXPERTS // EXP_DEV
    slot_rows = owners * CAP
    blocks = TOKENS // TOK_DEV
    in_window = (routes % EXP_DEV) == 0
    target = (routes // EXP_DEV).astype(jnp.int32)
    owner_ids = jnp.arange(owners, dtype=jnp.int32)
    routed = jnp.sum(((target[:, :, None] == owner_ids[None, None, :]) & in_window[:, :, None]).astype(jnp.int32), axis=1)
    routed = routed.reshape(blocks, TOK_DEV, owners)
    before = (jnp.cumsum(routed, axis=1) - routed).reshape(TOKENS, owners)
    position = jnp.take_along_axis(before, target, axis=1)
    retained = in_window & (position < CAP)
    token_ids = jnp.arange(TOKENS, dtype=jnp.int32)
    group_of = token_ids // (TOK_DEV * owners)
    source = (token_ids // TOK_DEV) % owners
    slot_total = N_DP * owners * slot_rows
    slot_index = ((group_of[:, None] * owners + target) * owners + source[:, None]) * CAP + position
    slot_index = jnp.where(retained, slot_index, slot_total).astype(jnp.int32)
    flat_index = slot_index.reshape(-1)
    holders = jnp.full((slot_total,), -1, jnp.int32).at[flat_index].set(
        jnp.broadcast_to(token_ids[:, None], slot_index.shape).reshape(-1), mode="drop")
    weight_of = jnp.zeros((slot_total,), jnp.float32).at[flat_index].set(
        probs.astype(jnp.float32).reshape(-1), mode="drop")
    holders = holders.reshape(N_DP, owners, slot_rows).transpose(1, 0, 2)
    weight_of = weight_of.reshape(N_DP, owners, slot_rows).transpose(1, 0, 2)
    gates = saved_gate.reshape(N_DP, owners, slot_rows, FF).transpose(1, 0, 2, 3)
    ups = saved_up.reshape(N_DP, owners, slot_rows, FF).transpose(1, 0, 2, 3)

    def one_expert(pieces):
        held, weight, gate_pre, up_pre, matrix = pieces
        filled = held >= 0
        safe_rows = jnp.maximum(held, 0)
        rows_x = jnp.where(filled[..., None], tokens[safe_rows], jnp.zeros((), tokens.dtype))
        rows_dy = jnp.where(filled[..., None], out_grad[safe_rows], jnp.zeros((), out_grad.dtype))
        gate_act = jax.nn.silu(gate_pre.astype(jnp.float32))
        hidden = (gate_act * up_pre.astype(jnp.float32)).astype(jnp.bfloat16)
        back_grad = jnp.einsum("grd,fd->grf", rows_dy.astype(jnp.float32), matrix.astype(jnp.float32))
        slot_grad = jnp.sum(hidden.astype(jnp.float32) * back_grad, axis=-1)
        scaled = (weight[..., None] * rows_dy.astype(jnp.float32)).astype(jnp.bfloat16)
        grad_pre = (weight[..., None] * back_grad * gate_act).astype(jnp.bfloat16)
        down_grad = jnp.einsum("grf,grd->fd", hidden.astype(jnp.float32), scaled.astype(jnp.float32))
        up_terms = jnp.einsum("grd,grf->gdf", rows_x.astype(jnp.float32), grad_pre.astype(jnp.float32))
        up_terms = lax.optimization_barrier(up_terms.astype(jnp.bfloat16)).astype(jnp.float32)
        up_grad = jnp.sum(up_terms, axis=0).astype(jnp.bfloat16)
        return down_grad, up_grad, slot_grad

    grad_down, grad_up, slot_grad = lax.map(one_expert, (holders, weight_of, gates, ups, down_weight))
    slot_flat = slot_grad.transpose(1, 0, 2).reshape(-1)
    prob_grad = jnp.where(retained, slot_flat[jnp.minimum(slot_index, slot_total - 1)], jnp.zeros((), jnp.float32))
    return grad_down, grad_up, prob_grad.astype(jnp.float32)
```

```python
import jax
import jax.numpy as jnp
from jax import lax
from jax.experimental import pallas as pl
from jax.experimental.pallas import tpu as pltpu
from jax.sharding import PartitionSpec as P

MESH = pl.DeviceIdType.MESH
NZ, NX, NY = 8, 4, 4
TOK = 128
CAP = 16
EXP_DEV = 4
D = 4096
FF = 768
NC = 4
DC = D // NC
UNITS = 2 * NC
ROWS = NX * CAP
SLOTS = NZ * ROWS
BLK = FF // (2 * NY)
F32 = jnp.float32
BF16 = jnp.bfloat16


def kernel(
    x_hbm, dy_hbm, probs_ref, routes_ref, gate_hbm, up_hbm, w_hbm,
    down_ref, upo_ref, pg_ref,
    tok, stg, recv, part, exr, yr, wv, gatev, hid, bg, lhs, sel, meta, metar, sg1, sg1r, sg2, sg2r,
    ld, zs, zr, xs, xr, es, er, ys, yrs, misc, cx, cy,
):
    dp = lax.axis_index("dp")
    e = lax.axis_index("expert")
    y, core = lax.div(dp, 2), lax.rem(dp, 2)
    z, x = lax.div(e, NX), lax.rem(e, NX)

    def at_z(zz):
        return (dp, lax.rem(zz, NZ) * NX + x)

    def at_x(xx):
        return (dp, z * NX + lax.rem(xx, NX))

    def at_y(yy):
        return (lax.rem(yy, NY) * 2 + core, e)

    partner = (y * 2 + 1 - core, e)

    def remote(src, dst, send, recv_sem, dev):
        return pltpu.make_async_remote_copy(
            src_ref=src, dst_ref=dst, send_sem=send, recv_sem=recv_sem,
            device_id=dev, device_id_type=MESH,
        )

    def drain(ref, sem):
        pltpu.make_async_copy(ref, ref, sem).wait()

    barrier = pltpu.get_barrier_semaphore()

    def greet(dev):
        pl.semaphore_signal(barrier, inc=1, device_id=dev, device_id_type=MESH)

    for i in range(1, NZ):
        greet(at_z(z + i))
    for i in range(1, NX):
        greet(at_x(x + i))
    for i in range(1, NY):
        greet(at_y(y + i))
    greet(partner)

    dy_loads = [
        pltpu.make_async_copy(dy_hbm.at[:, c * DC:(c + 1) * DC], tok.at[c, 0], ld.at[c])
        for c in range(NC)
    ]
    step = D // 8
    sub = step // NC
    x_loads = [
        pltpu.make_async_copy(
            x_hbm.at[:, d * step + c * sub:d * step + (c + 1) * sub],
            tok.at[NC + c, 0, :, d * sub:(d + 1) * sub],
            ld.at[NC + c],
        )
        for c in range(NC)
        for d in range(8)
    ]
    g_load = pltpu.make_async_copy(gate_hbm, gatev, ld.at[UNITS])
    u_load = pltpu.make_async_copy(up_hbm, hid, ld.at[UNITS + 1])
    w_load = pltpu.make_async_copy(w_hbm, wv, ld.at[UNITS + 2])
    for c in dy_loads:
        c.start()
    g_load.start()
    u_load.start()
    for c in x_loads:
        c.start()
    w_load.start()

    def zcopy(u, src, dst, sign):
        way = sign * (1 - 2 * lax.rem(u, 2))
        return remote(tok.at[u, src], tok.at[u, dst], zs.at[u], zr.at[u, dst], at_z(z + NZ + way))

    def send_own(u):
        zcopy(u, 0, 1, 1).start()
        zcopy(u, 0, NZ - 1, -1).start()

    r = routes_ref[...]
    p = probs_ref[...].astype(F32)
    owners = NZ * NX
    wid = lax.broadcasted_iota(jnp.int32, (owners, TOK), 0) * EXP_DEV
    routed = jnp.zeros((owners, TOK), F32)
    weight = jnp.zeros((owners, TOK), F32)
    for k in range(8):
        hit = wid == r[k:k + 1, :]
        routed = jnp.where(hit, 1.0, routed)
        weight = jnp.where(hit, p[k:k + 1, :], weight)
    earlier = lax.broadcasted_iota(jnp.int32, (TOK, TOK), 0) < lax.broadcasted_iota(
        jnp.int32, (TOK, TOK), 1
    )
    before = jnp.dot(
        routed.astype(BF16), jnp.where(earlier, 1.0, 0.0).astype(BF16), preferred_element_type=F32
    )
    pos = jnp.where((routed > 0.0) & (before < float(CAP)), before, -1.0)
    for i in range(NZ):
        meta[i, 0:NX, :] = pos[i * NX:(i + 1) * NX]
        meta[i, NX:2 * NX, :] = weight[i * NX:(i + 1) * NX]
    metar[z] = meta[z]

    pl.semaphore_wait(barrier, NZ + NX + NY - 2)
    dy_loads[0].wait()
    send_own(0)
    for i in range(1, NZ):
        to = lax.rem(z + i, NZ)
        remote(meta.at[to], metar.at[z], misc.at[0], misc.at[1], at_z(to)).start()
    dy_loads[1].wait()
    send_own(1)
    for c in dy_loads[2:]:
        c.wait()
    g_load.wait()
    u_load.wait()

    gate = gatev[...].astype(F32)
    act = gate / (1.0 + jnp.exp(-gate))
    hidden = (act * hid[...].astype(F32)).astype(BF16)
    hid[...] = hidden
    lhs[0] = hidden.T
    bg[...] = jnp.zeros_like(bg)
    for c in range(NC):
        drain(tok.at[NC + c, 0], ld.at[NC + c])
    w_load.wait()

    drain(metar.at[0:NZ - 1], misc.at[1])
    slot_pos = lax.broadcasted_iota(jnp.int32, (NX, CAP, TOK), 1).astype(F32)

    def build(src, carry):
        m = metar[src]
        at = m[0:NX].reshape(NX, 1, TOK)
        wt = m[NX:2 * NX].reshape(NX, 1, TOK)
        hit = jnp.broadcast_to(at, (NX, CAP, TOK)) == slot_pos
        one = jnp.where(hit, 1.0, 0.0)
        wtd = jnp.where(hit, jnp.broadcast_to(wt, (NX, CAP, TOK)), 0.0)
        sel[0, src] = wtd.reshape(ROWS, TOK).astype(BF16)
        sel[1, src] = one.reshape(ROWS, TOK).astype(BF16)
        return carry

    lax.fori_loop(0, NZ, build, 0)

    def select(u, j):
        way = 1 - 2 * lax.rem(u, 2)
        src = lax.rem(z + 8 * NZ - way * j, NZ)
        s = sel[lax.div(u, NC), src]
        rows = jnp.dot(s, tok[u, j], preferred_element_type=F32).astype(BF16)
        stg[u, j] = rows.reshape(NX, CAP, DC)
        slot = src * NX + x
        recv[u, slot] = stg[u, j, x]
        for i in range(1, NX):
            to = lax.rem(x + i, NX)
            remote(stg.at[u, j, to], recv.at[u, slot], xs.at[u], xr.at[u], at_x(to)).start()

    def on(k, t, body):
        u = k - t

        @pl.when((u >= 0) & (u < UNITS))
        def _():
            body(u)

    def relay1(u):
        drain(tok.at[u, 1], zr.at[u, 1])
        zcopy(u, 1, 2, 1).start()
        drain(tok.at[u, 7], zr.at[u, 7])
        zcopy(u, 7, 6, -1).start()

    def relay2(u):
        drain(tok.at[u, 2], zr.at[u, 2])
        zcopy(u, 2, 3, 1).start()
        drain(tok.at[u, 6], zr.at[u, 6])
        zcopy(u, 6, 5, -1).start()

    def relay3(u):
        drain(tok.at[u, 3], zr.at[u, 3])
        zcopy(u, 3, 4, 1).start()

    def pick1(u):
        select(u, 0)
        select(u, 1)
        select(u, 7)

    def pick2(u):
        select(u, 2)
        select(u, 6)

    def pick3(u):
        select(u, 3)
        drain(tok.at[u, 5], zr.at[u, 5])
        select(u, 5)

    def pick4(u):
        drain(tok.at[u, 4], zr.at[u, 4])
        select(u, 4)

    def compute(u):
        c = lax.rem(u, NC)
        kind = lax.div(u, NC)
        drain(recv.at[u, 0:NZ * (NX - 1)], xr.at[u])

        @pl.when(kind == 0)
        def _():
            a = recv[u].reshape(SLOTS, DC)
            wc = wv[:, pl.ds(pl.multiple_of(c * DC, DC), DC)]
            bg[...] += lax.dot_general(
                a, wc, (((1,), (1,)), ((), ())), preferred_element_type=F32
            )

        def tile(n, carry):
            cols = recv[u, :, :, pl.ds(pl.multiple_of(n * 256, 256), 256)].reshape(SLOTS, 256)
            prod = jnp.dot(lhs[kind], cols, preferred_element_type=F32).astype(BF16)

            @pl.when(kind == 0)
            def _():
                for d in range(2 * NY):
                    for h in range(2):
                        part[c, d % 2, d // 2, pl.ds(pl.multiple_of((2 * n + h) * BLK, BLK), BLK), :] = (
                            prod[d * BLK:(d + 1) * BLK, h * 128:(h + 1) * 128]
                        )

            @pl.when(kind == 1)
            def _():
                part[c, 0, n] = prod[:, 0:128]
                part[c, 1, n] = prod[:, 128:256]

            return carry

        lax.fori_loop(0, NY, tile, 0)

        @pl.when(kind == 1)
        def _():
            pl.semaphore_wait(cx.at[c], 1)

        remote(part.at[c, 1 - core], exr.at[c], es.at[u], er.at[u], partner).start()

        @pl.when(u == NC - 1)
        def _():
            back = bg[...]
            g = gatev[...].astype(F32)
            pre = (back * (g / (1.0 + jnp.exp(-g)))).astype(BF16)
            lhs[1] = pre.T
            sg = jnp.sum(hid[...].astype(F32) * back, axis=1, keepdims=True)
            lane = lax.broadcasted_iota(jnp.int32, (SLOTS, TOK), 1)
            row = lax.broadcasted_iota(jnp.int32, (SLOTS, TOK), 0)
            spread = jnp.where(lane == x * CAP + lax.rem(row, CAP), sg, 0.0)
            packed = jnp.sum(spread.reshape(NZ * NX, CAP, TOK), axis=1)
            for s in range(NZ * NX):
                sg1[s % NX, s // NX:s // NX + 1, :] = packed[s:s + 1, :]
            sg1r[x] = sg1[x]
            for i in range(1, NX):
                to = lax.rem(x + i, NX)
                remote(sg1.at[to], sg1r.at[x], misc.at[2], misc.at[3], at_x(to)).start()

    def chip_sum(u):
        c = lax.rem(u, NC)
        drain(exr.at[c], er.at[u])

        @pl.when(u >= NC)
        def _():
            pl.semaphore_wait(cy.at[c], NY - 1)

        for i in range(1, NY):
            to = lax.rem(y + i, NY)
            part[c, core, to] = (
                part[c, core, to].astype(F32) + exr[c, to].astype(F32)
            ).astype(BF16)
            remote(part.at[c, core, to], yr.at[c, i - 1], ys.at[u], yrs.at[u], at_y(to)).start()

    def finish(u):
        c = lax.rem(u, NC)
        drain(yr.at[c], yrs.at[u])
        total = part[c, core, y].astype(F32) + exr[c, y].astype(F32)
        for i in range(NY - 1):
            total = total + yr[c, i].astype(F32)

        @pl.when(u < NC)
        def _():
            for i in range(DC // 128):
                down_ref[:, pl.ds(pl.multiple_of(c * DC + i * 128, 128), 128)] = (
                    total[i * BLK:(i + 1) * BLK]
                )
            pl.semaphore_signal(cx.at[c], inc=1, device_id=partner, device_id_type=MESH)
            for i in range(1, NY):
                pl.semaphore_signal(cy.at[c], inc=1, device_id=at_y(y + i), device_id_type=MESH)

        @pl.when(u >= NC)
        def _():
            upo_ref[pl.ds(pl.multiple_of(c * 128, 128), 128), :] = total.T.astype(BF16)

        drain(tok.at[u, 0:NZ - 1], zs.at[u])
        drain(recv.at[u, 0:NZ * (NX - 1)], xs.at[u])
        drain(part.at[c, 0], es.at[u])
        drain(yr.at[c], ys.at[u])

    def grads_over_z():
        drain(sg1r.at[0:NX - 1], misc.at[3])
        both = sg1r[0] + sg1r[1] + sg1r[2] + sg1r[3]
        for i in range(NZ):
            sg2[i] = jnp.broadcast_to(both[i:i + 1, :], (8, TOK))
        sg2r[z] = sg2[z]
        for i in range(1, NZ):
            to = lax.rem(z + i, NZ)
            remote(sg2.at[to], sg2r.at[z], misc.at[4], misc.at[5], at_z(to)).start()

    def grads_out():
        drain(sg2r.at[0:NZ - 1], misc.at[5])
        eye = lax.broadcasted_iota(jnp.int32, (TOK, TOK), 0) == lax.broadcasted_iota(
            jnp.int32, (TOK, TOK), 1
        )
        rr = routes_ref[...]
        total = jnp.zeros((8, TOK), F32)
        for i in range(NZ):
            spread = jnp.where(eye, jnp.broadcast_to(sg2r[i, 0:1, :], (TOK, TOK)), 0.0)
            column = jnp.sum(spread, axis=1, keepdims=True)[0:ROWS].reshape(NX, CAP, 1)
            at = meta[i, 0:NX, :].reshape(NX, 1, TOK)
            hit = jnp.broadcast_to(at, (NX, CAP, TOK)) == slot_pos
            got = jnp.sum(jnp.where(hit, column, 0.0), axis=1)
            for j in range(NX):
                total = jnp.where(rr == (i * NX + j) * EXP_DEV, got[j:j + 1, :], total)
        pg_ref[...] = total / probs_ref[...].astype(F32)
        drain(meta.at[0:NZ - 1], misc.at[0])
        drain(sg1.at[0:NX - 1], misc.at[2])
        drain(sg2.at[0:NZ - 1], misc.at[4])

    def body(k, carry):
        @pl.when(k + 2 < UNITS)
        def _():
            send_own(k + 2)

        on(k, 1, relay1)
        on(k, 2, relay2)
        on(k, 3, relay3)
        on(k, 1, pick1)
        on(k, 2, pick2)
        on(k, 3, pick3)
        on(k, 4, pick4)
        on(k, 5, compute)
        on(k, 6, chip_sum)
        on(k, 7, finish)

        @pl.when(k == NC + 5)
        def _():
            grads_over_z()

        @pl.when(k == NC + 6)
        def _():
            grads_out()

        return carry

    lax.fori_loop(0, UNITS + 7, body, 0)


def per_device(tokens, out_grad, probs, routes, saved_gate, saved_up, down_weight):
    anyspace = pl.BlockSpec(memory_space=pl.ANY)
    vmem = pl.BlockSpec(memory_space=pltpu.VMEM)
    dma = pltpu.SemaphoreType.DMA
    down, up, pg = pl.pallas_call(
        kernel,
        out_shape=(
            jax.ShapeDtypeStruct((BLK, D), F32),
            jax.ShapeDtypeStruct((D // 8, FF), BF16),
            jax.ShapeDtypeStruct((8, TOK), F32),
        ),
        in_specs=[anyspace, anyspace, vmem, vmem, anyspace, anyspace, anyspace],
        out_specs=(vmem, vmem, vmem),
        scratch_shapes=[
            pltpu.VMEM((UNITS, NZ, TOK, DC), BF16),
            pltpu.VMEM((UNITS, NZ, NX, CAP, DC), BF16),
            pltpu.VMEM((UNITS, NZ * NX, CAP, DC), BF16),
            pltpu.VMEM((NC, 2, NY, FF, 128), BF16),
            pltpu.VMEM((NC, NY, FF, 128), BF16),
            pltpu.VMEM((NC, NY - 1, FF, 128), BF16),
            pltpu.VMEM((FF, D), BF16),
            pltpu.VMEM((SLOTS, FF), BF16),
            pltpu.VMEM((SLOTS, FF), BF16),
            pltpu.VMEM((SLOTS, FF), F32),
            pltpu.VMEM((2, FF, SLOTS), BF16),
            pltpu.VMEM((2, NZ, ROWS, TOK), BF16),
            pltpu.VMEM((NZ, 8, TOK), F32),
            pltpu.VMEM((NZ, 8, TOK), F32),
            pltpu.VMEM((NX, NZ, TOK), F32),
            pltpu.VMEM((NX, NZ, TOK), F32),
            pltpu.VMEM((NZ, 8, TOK), F32),
            pltpu.VMEM((NZ, 8, TOK), F32),
            dma((UNITS + 3,)),
            dma((UNITS,)),
            dma((UNITS, NZ)),
            dma((UNITS,)),
            dma((UNITS,)),
            dma((UNITS,)),
            dma((UNITS,)),
            dma((UNITS,)),
            dma((UNITS,)),
            dma((6,)),
            pltpu.SemaphoreType.REGULAR((NC,)),
            pltpu.SemaphoreType.REGULAR((NC,)),
        ],
        compiler_params=pltpu.CompilerParams(
            collective_id=0, has_side_effects=True, vmem_limit_bytes=67043328
        ),
        name="expert_grads",
    )(
        tokens, out_grad, probs.T, routes.T, saved_gate, saved_up,
        down_weight.reshape(down_weight.shape[1:]),
    )
    return down[None], up[None], pg.T


def solution(mesh):
    rows = P(("dp", "expert"), None)
    return jax.shard_map(
        per_device,
        mesh=mesh,
        in_specs=(rows, rows, rows, rows, rows, rows, P("expert", None, None)),
        out_specs=(P("expert", "dp", None), P("expert", "dp", None), rows),
        check_vma=False,
    )
```

```python
import jax
import jax.numpy as jnp
from jax import lax
from jax.experimental import pallas as pl
from jax.experimental.pallas import tpu as pltpu
from jax.sharding import PartitionSpec as P

MESH = pl.DeviceIdType.MESH
NZ, NX, NY = 8, 4, 4
TOK = 128
CAP = 16
EXP_DEV = 4
D = 4096
FF = 768
NC = 8
DC = D // NC
UNITS = 2 * NC
ROWS = NX * CAP
SLOTS = NZ * ROWS
BLK = FF // (2 * NY)
HALF = FF // 2
AHEAD = 2
F32 = jnp.float32
BF16 = jnp.bfloat16


def kernel(
    x_hbm, dy_hbm, probs_ref, routes_ref, gate_hbm, up_hbm, w_hbm,
    down_hbm, up_out, pg_ref,
    tok, far, stg, stf, recv, part, exr, yr, wv, gatev, hid, bg, lhs, sel, meta, metar, metaf, sg1, sg1r, sg2, sg2r,
    down_ref, upo_ref, ld, od, zs, zr, xs, xr, es, er, ys, yrs, misc, cx, cy,
):
    dp = lax.axis_index("dp")
    e = lax.axis_index("expert")
    y, core = lax.div(dp, 2), lax.rem(dp, 2)
    z, x = lax.div(e, NX), lax.rem(e, NX)

    def at_z(zz):
        return (dp, lax.rem(zz, NZ) * NX + x)

    def at_x(xx):
        return (dp, z * NX + lax.rem(xx, NX))

    def at_y(yy):
        return (lax.rem(yy, NY) * 2 + core, e)

    partner = (y * 2 + 1 - core, e)

    def remote(src, dst, send, recv_sem, dev):
        return pltpu.make_async_remote_copy(
            src_ref=src, dst_ref=dst, send_sem=send, recv_sem=recv_sem,
            device_id=dev, device_id_type=MESH,
        )

    def drain(ref, sem):
        pltpu.make_async_copy(ref, ref, sem).wait()

    barrier = pltpu.get_barrier_semaphore()

    def greet(dev):
        pl.semaphore_signal(barrier, inc=1, device_id=dev, device_id_type=MESH)

    for i in range(1, NZ):
        greet(at_z(z + i))
    for i in range(1, NX):
        greet(at_x(x + i))
    for i in range(1, NY):
        greet(at_y(y + i))
    greet(partner)

    dy_loads = [
        pltpu.make_async_copy(dy_hbm.at[:, c * DC:(c + 1) * DC], tok.at[c, 0], ld.at[c])
        for c in range(NC)
    ]
    step = D // 8
    x_loads = [
        pltpu.make_async_copy(
            x_hbm.at[:, (2 * i + c % 2) * step + c // 2 * 128:(2 * i + c % 2) * step + (c // 2 + 1) * 128],
            tok.at[NC + c, 0, :, i * 128:(i + 1) * 128],
            ld.at[NC + c],
        )
        for c in range(NC)
        for i in range(NY)
    ]
    g_load = pltpu.make_async_copy(gate_hbm, gatev, ld.at[UNITS])
    u_load = pltpu.make_async_copy(up_hbm, hid, ld.at[UNITS + 1])
    w_load = pltpu.make_async_copy(w_hbm, wv, ld.at[UNITS + 2])
    for c in dy_loads:
        c.start()
    g_load.start()
    u_load.start()
    for c in x_loads:
        c.start()
    w_load.start()

    def zcopy(u, src, dst, sign):
        way = sign * (1 - 2 * lax.rem(u, 2))
        return remote(tok.at[u, src], tok.at[u, dst], zs.at[u], zr.at[u, dst], at_z(z + NZ + way))

    def zfar(u, src, dst, sign):
        way = sign * (1 - 2 * lax.rem(u, 2))
        i = dst - 4
        c = lax.rem(u, NC)
        s = sel[lax.div(u, NC), NZ + 2 * lax.rem(u, 2) + i]
        rows = jnp.dot(s, tok[u, src], preferred_element_type=F32).astype(BF16)
        far[c, i] = rows.reshape(NX, CAP, DC)
        remote(far.at[c, i], stf.at[u, i], zs.at[u], zr.at[u, 2 + dst], at_z(z + NZ + way)).start()

    def send_own(u):
        zcopy(u, 0, 1, 1).start()
        zcopy(u, 0, 5, -1).start()

    r = routes_ref[...]
    p = probs_ref[...].astype(F32)
    owners = NZ * NX
    wid = lax.broadcasted_iota(jnp.int32, (owners, TOK), 0) * EXP_DEV
    routed = jnp.zeros((owners, TOK), F32)
    weight = jnp.zeros((owners, TOK), F32)
    for k in range(8):
        hit = wid == r[k:k + 1, :]
        routed = jnp.where(hit, 1.0, routed)
        weight = jnp.where(hit, p[k:k + 1, :], weight)
    earlier = lax.broadcasted_iota(jnp.int32, (TOK, TOK), 0) < lax.broadcasted_iota(
        jnp.int32, (TOK, TOK), 1
    )
    before = jnp.dot(
        routed.astype(BF16), jnp.where(earlier, 1.0, 0.0).astype(BF16), preferred_element_type=F32
    )
    pos = jnp.where((routed > 0.0) & (before < float(CAP)), before, -1.0)
    for i in range(NZ):
        meta[i, 0:NX, :] = pos[i * NX:(i + 1) * NX]
        meta[i, NX:2 * NX, :] = weight[i * NX:(i + 1) * NX]
    metar[z] = meta[z]

    pl.semaphore_wait(barrier, NZ + NX + NY - 2)
    for i in range(1, NZ):
        to = lax.rem(z + i, NZ)
        remote(meta.at[to], metar.at[z], misc.at[0], misc.at[1], at_z(to)).start()
    for i, (node, plane) in enumerate(((3, 4), (6, 5), (5, 4), (2, 3))):
        plane = lax.rem(z + plane, NZ)
        remote(meta.at[plane], metaf.at[i], misc.at[6], misc.at[7], at_z(z + node)).start()
    for c in range(NC):
        dy_loads[c].wait()
        if c < max(AHEAD, 1):
            send_own(c)
    g_load.wait()
    u_load.wait()

    gate = gatev[...].astype(F32)
    act = gate / (1.0 + jnp.exp(-gate))
    hidden = (act * hid[...].astype(F32)).astype(BF16)
    hid[...] = hidden
    lhs[0] = hidden.T
    bg[...] = jnp.zeros_like(bg)
    for c in range(NC):
        drain(tok.at[NC + c, 0], ld.at[NC + c])
    w_load.wait()

    drain(metar.at[0:NZ - 1], misc.at[1])
    drain(metaf, misc.at[7])
    slot_pos = lax.broadcasted_iota(jnp.int32, (NX, CAP, TOK), 1).astype(F32)

    def build(m, i):
        at = m[0:NX].reshape(NX, 1, TOK)
        wt = m[NX:2 * NX].reshape(NX, 1, TOK)
        hit = jnp.broadcast_to(at, (NX, CAP, TOK)) == slot_pos
        one = jnp.where(hit, 1.0, 0.0)
        wtd = jnp.where(hit, jnp.broadcast_to(wt, (NX, CAP, TOK)), 0.0)
        sel[0, i] = wtd.reshape(ROWS, TOK).astype(BF16)
        sel[1, i] = one.reshape(ROWS, TOK).astype(BF16)

    for i in range(NZ):
        build(metar[i], i)
    for i in range(4):
        build(metaf[i], NZ + i)

    def pick(u, j):
        way = 1 - 2 * lax.rem(u, 2)
        src = lax.rem(z + 8 * NZ - way * j, NZ)
        c = lax.rem(u, NC)
        i = j if j < 4 else j - 2
        s = sel[lax.div(u, NC), src]
        rows = jnp.dot(s, tok[u, i], preferred_element_type=F32).astype(BF16)
        stg[c, i] = rows.reshape(NX, CAP, DC)
        spread(u, j, stg.at[c, i])

    def spread(u, j, ref):
        way = 1 - 2 * lax.rem(u, 2)
        src = lax.rem(z + 8 * NZ - way * j, NZ)
        slot = src * NX + x
        recv[u, slot] = ref[x]
        for i in range(1, NX):
            to = lax.rem(x + i, NX)
            remote(ref.at[to], recv.at[u, slot], xs.at[u], xr.at[u], at_x(to)).start()

    def on(k, t, body):
        u = k - t

        @pl.when((u >= 0) & (u < UNITS))
        def _():
            body(u)

    def relay1(u):
        drain(tok.at[u, 1], zr.at[u, 1])
        zcopy(u, 1, 2, 1).start()
        drain(tok.at[u, 5], zr.at[u, 5])
        zcopy(u, 5, 4, -1).start()

    def relay2(u):
        drain(tok.at[u, 2], zr.at[u, 2])
        zcopy(u, 2, 3, 1).start()
        drain(tok.at[u, 4], zr.at[u, 4])
        zfar(u, 4, 5, -1)

    def relay3(u):
        drain(tok.at[u, 3], zr.at[u, 3])
        zfar(u, 3, 4, 1)

    def pick1(u):
        pick(u, 0)
        pick(u, 1)
        pick(u, 7)

    def pick2(u):
        pick(u, 2)
        pick(u, 6)

    def pick3(u):
        pick(u, 3)
        drain(stf.at[u, 1], zr.at[u, 7])
        spread(u, 5, stf.at[u, 1])

    def pick4(u):
        drain(stf.at[u, 0], zr.at[u, 6])
        spread(u, 4, stf.at[u, 0])

    def compute(u):
        c = lax.rem(u, NC)
        kind = lax.div(u, NC)
        drain(recv.at[u, 0:NZ * (NX - 1)], xr.at[u])

        @pl.when(kind == 0)
        def _():
            a = recv[u].reshape(SLOTS, DC)
            wc = wv[:, pl.ds(pl.multiple_of(c * DC, DC), DC)]
            bg[...] += lax.dot_general(
                a, wc, (((1,), (1,)), ((), ())), preferred_element_type=F32
            )

        def tile(n, carry):
            cols = recv[u, :, :, pl.ds(pl.multiple_of(n * 256, 256), 256)].reshape(SLOTS, 256)
            prod = jnp.dot(lhs[kind], cols, preferred_element_type=F32).astype(BF16)

            @pl.when(kind == 0)
            def _():
                for d in range(2 * NY):
                    for h in range(2):
                        part[c, d % 2 * NY + d // 2, pl.ds(pl.multiple_of((2 * n + h) * BLK, BLK), BLK), :] = (
                            prod[d * BLK:(d + 1) * BLK, h * 128:(h + 1) * 128]
                        )

            @pl.when(kind == 1)
            def _():
                for i in range(2):
                    for h in range(2):
                        part[c, 4 * n + 2 * i + h] = (
                            prod[h * HALF:(h + 1) * HALF, i * 128:(i + 1) * 128]
                        )

                @pl.when(core != lax.rem(c, 2))
                def _():
                    for i in range(2):
                        m = 2 * n + i
                        ref = pl.ds(2 * m, 2)
                        remote(part.at[c, ref], exr.at[c, ref], es.at[u], er.at[u, m], partner).start()

            return carry

        @pl.when(kind == 1)
        def _():
            pl.semaphore_wait(cx.at[c], 1)

        lax.fori_loop(0, DC // 256, tile, 0)

        @pl.when(kind == 0)
        def _():
            for m in range(NY):
                remote(
                    part.at[c, (1 - core) * NY + m], exr.at[c, m], es.at[u], er.at[u, m], partner
                ).start()

        @pl.when(u == NC - 1)
        def _():
            back = bg[...]
            g = gatev[...].astype(F32)
            pre = (back * (g / (1.0 + jnp.exp(-g)))).astype(BF16)
            lhs[1] = pre.T
            sg = jnp.sum(hid[...].astype(F32) * back, axis=1, keepdims=True)
            lane = lax.broadcasted_iota(jnp.int32, (SLOTS, TOK), 1)
            row = lax.broadcasted_iota(jnp.int32, (SLOTS, TOK), 0)
            spread = jnp.where(lane == x * CAP + lax.rem(row, CAP), sg, 0.0)
            packed = jnp.sum(spread.reshape(NZ * NX, CAP, TOK), axis=1)
            for s in range(NZ * NX):
                sg1[s % NX, s // NX:s // NX + 1, :] = packed[s:s + 1, :]
            sg1r[x] = sg1[x]
            for i in range(1, NX):
                to = lax.rem(x + i, NX)
                remote(sg1.at[to], sg1r.at[x], misc.at[2], misc.at[3], at_x(to)).start()

    def chip_sum(u):
        c = lax.rem(u, NC)
        drain(tok.at[u, 0:6], zs.at[u])
        drain(recv.at[u, 0:NZ * (NX - 1)], xs.at[u])

        @pl.when(u < NC)
        def _():
            for i in (2, 3, 1):
                to = lax.rem(y + i, NY)
                mine = core * NY + to
                drain(exr.at[c, to], er.at[u, to])
                part[c, mine] = (part[c, mine].astype(F32) + exr[c, to].astype(F32)).astype(BF16)
                remote(part.at[c, mine], yr.at[c, i - 1, 0], ys.at[u], yrs.at[u], at_y(to)).start()

        @pl.when(u >= NC)
        def _():
            pl.semaphore_wait(cy.at[c], NY - 1)

        @pl.when((u >= NC) & (core == lax.rem(c, 2)))
        def _():
            for i in (2, 3, 1):
                to = lax.rem(y + i, NY)
                ref = pl.ds(2 * to, 2)
                drain(exr.at[c, ref], er.at[u, to])
                for h in range(2):
                    m = 2 * to + h
                    part[c, m] = (part[c, m].astype(F32) + exr[c, m].astype(F32)).astype(BF16)
                remote(part.at[c, ref], yr.at[c, i - 1], ys.at[u], yrs.at[u], at_y(to)).start()

    def finish(u):
        c = lax.rem(u, NC)
        own = core == lax.rem(c, 2)

        @pl.when(u < NC)
        def _():
            drain(exr.at[c, y], er.at[u, y])
            drain(part.at[c, 0:NY - 1], yrs.at[u])
            total = part[c, core * NY + y].astype(F32) + exr[c, y].astype(F32)
            for i in range(NY - 1):
                total = total + yr[c, i, 0].astype(F32)
            for i in range(DC // 128):
                down_ref[:, pl.ds(pl.multiple_of(c * DC + i * 128, 128), 128)] = (
                    total[i * BLK:(i + 1) * BLK]
                )
            cols = pl.ds(pl.multiple_of(c * DC, DC), DC)
            pltpu.make_async_copy(down_ref.at[:, cols], down_hbm.at[:, cols], od.at[u]).start()
            pl.semaphore_signal(cx.at[c], inc=1, device_id=partner, device_id_type=MESH)
            for i in range(1, NY):
                pl.semaphore_signal(cy.at[c], inc=1, device_id=at_y(y + i), device_id_type=MESH)
            drain(part.at[c, 0:NY], es.at[u])
            drain(part.at[c, 0:NY - 1], ys.at[u])

        @pl.when((u >= NC) & own)
        def _():
            drain(exr.at[c, pl.ds(2 * y, 2)], er.at[u, y])
            drain(yr.at[c], yrs.at[u])
            for h in range(2):
                total = part[c, 2 * y + h].astype(F32) + exr[c, 2 * y + h].astype(F32)
                for i in range(NY - 1):
                    total = total + yr[c, i, h].astype(F32)
                upo_ref[
                    pl.ds(pl.multiple_of(lax.div(c, 2) * 128, 128), 128), h * HALF:(h + 1) * HALF
                ] = total.T.astype(BF16)
            out = pl.ds(pl.multiple_of(lax.div(c, 2) * 128, 128), 128)
            pltpu.make_async_copy(upo_ref.at[out], up_out.at[out], od.at[u]).start()
            drain(yr.at[c], ys.at[u])

        @pl.when((u >= NC) & (core != lax.rem(c, 2)))
        def _():
            drain(part.at[c], es.at[u])

    def grads_over_z():
        drain(sg1r.at[0:NX - 1], misc.at[3])
        both = sg1r[0] + sg1r[1] + sg1r[2] + sg1r[3]
        for i in range(NZ):
            sg2[i] = jnp.broadcast_to(both[i:i + 1, :], (8, TOK))
        sg2r[z] = sg2[z]
        for i in range(1, NZ):
            to = lax.rem(z + i, NZ)
            remote(sg2.at[to], sg2r.at[z], misc.at[4], misc.at[5], at_z(to)).start()

    def grads_out():
        drain(sg2r.at[0:NZ - 1], misc.at[5])
        eye = lax.broadcasted_iota(jnp.int32, (TOK, TOK), 0) == lax.broadcasted_iota(
            jnp.int32, (TOK, TOK), 1
        )
        rr = routes_ref[...]
        total = jnp.zeros((8, TOK), F32)
        for i in range(NZ):
            spread = jnp.where(eye, jnp.broadcast_to(sg2r[i, 0:1, :], (TOK, TOK)), 0.0)
            column = jnp.sum(spread, axis=1, keepdims=True)[0:ROWS].reshape(NX, CAP, 1)
            at = meta[i, 0:NX, :].reshape(NX, 1, TOK)
            hit = jnp.broadcast_to(at, (NX, CAP, TOK)) == slot_pos
            got = jnp.sum(jnp.where(hit, column, 0.0), axis=1)
            for j in range(NX):
                total = jnp.where(rr == (i * NX + j) * EXP_DEV, got[j:j + 1, :], total)
        pg_ref[...] = total / probs_ref[...].astype(F32)
        drain(meta.at[0:NZ - 1], misc.at[0])
        drain(metaf, misc.at[6])
        drain(sg1.at[0:NX - 1], misc.at[2])
        drain(sg2.at[0:NZ - 1], misc.at[4])

    def body(k, carry):
        @pl.when((k + AHEAD < UNITS) & (k + AHEAD > 0))
        def _():
            send_own(k + AHEAD)

        on(k, 1, relay1)
        on(k, 2, relay2)
        on(k, 3, relay3)
        on(k, 1, pick1)
        on(k, 2, pick2)
        on(k, 3, pick3)
        on(k, 4, pick4)
        on(k, 5, compute)
        on(k, 7, chip_sum)
        on(k, 9, finish)

        @pl.when(k == NC + 5)
        def _():
            grads_over_z()

        @pl.when(k == NC + 6)
        def _():
            grads_out()

        return carry

    lax.fori_loop(0, UNITS + 9, body, 0)
    for c in range(NC):
        drain(down_ref.at[:, c * DC:(c + 1) * DC], od.at[c])
    for q in range(NC // 2):
        drain(upo_ref.at[q * 128:(q + 1) * 128], od.at[NC + 2 * q + core])


def per_device(tokens, out_grad, probs, routes, saved_gate, saved_up, down_weight):
    anyspace = pl.BlockSpec(memory_space=pl.ANY)
    vmem = pl.BlockSpec(memory_space=pltpu.VMEM)
    dma = pltpu.SemaphoreType.DMA
    down, up, pg = pl.pallas_call(
        kernel,
        out_shape=(
            jax.ShapeDtypeStruct((BLK, D), F32),
            jax.ShapeDtypeStruct((D // 8, FF), BF16),
            jax.ShapeDtypeStruct((8, TOK), F32),
        ),
        in_specs=[anyspace, anyspace, vmem, vmem, anyspace, anyspace, anyspace],
        out_specs=(anyspace, anyspace, vmem),
        scratch_shapes=[
            pltpu.VMEM((UNITS, 6, TOK, DC), BF16),
            pltpu.VMEM((NC, 2, NX, CAP, DC), BF16),
            pltpu.VMEM((NC, 6, NX, CAP, DC), BF16),
            pltpu.VMEM((UNITS, 2, NX, CAP, DC), BF16),
            pltpu.VMEM((UNITS, NZ * NX, CAP, DC), BF16),
            pltpu.VMEM((NC, 2 * NY, HALF, 128), BF16),
            pltpu.VMEM((NC, 2 * NY, HALF, 128), BF16),
            pltpu.VMEM((NC, NY - 1, 2, HALF, 128), BF16),
            pltpu.VMEM((FF, D), BF16),
            pltpu.VMEM((SLOTS, FF), BF16),
            pltpu.VMEM((SLOTS, FF), BF16),
            pltpu.VMEM((SLOTS, FF), F32),
            pltpu.VMEM((2, FF, SLOTS), BF16),
            pltpu.VMEM((2, NZ + 4, ROWS, TOK), BF16),
            pltpu.VMEM((NZ, 8, TOK), F32),
            pltpu.VMEM((NZ, 8, TOK), F32),
            pltpu.VMEM((4, 8, TOK), F32),
            pltpu.VMEM((NX, NZ, TOK), F32),
            pltpu.VMEM((NX, NZ, TOK), F32),
            pltpu.VMEM((NZ, 8, TOK), F32),
            pltpu.VMEM((NZ, 8, TOK), F32),
            pltpu.VMEM((BLK, D), F32),
            pltpu.VMEM((D // 8, FF), BF16),
            dma((UNITS + 3,)),
            dma((UNITS,)),
            dma((UNITS,)),
            dma((UNITS, NZ)),
            dma((UNITS,)),
            dma((UNITS,)),
            dma((UNITS,)),
            dma((UNITS, NY)),
            dma((UNITS,)),
            dma((UNITS,)),
            dma((8,)),
            pltpu.SemaphoreType.REGULAR((NC,)),
            pltpu.SemaphoreType.REGULAR((NC,)),
        ],
        compiler_params=pltpu.CompilerParams(
            collective_id=0, has_side_effects=True, vmem_limit_bytes=67043328
        ),
        name="expert_grads",
    )(
        tokens, out_grad, probs.T, routes.T, saved_gate, saved_up,
        down_weight.reshape(down_weight.shape[1:]),
    )
    return down[None], up[None], pg.T


def solution(mesh):
    rows = P(("dp", "expert"), None)
    return jax.shard_map(
        per_device,
        mesh=mesh,
        in_specs=(rows, rows, rows, rows, rows, rows, P("expert", None, None)),
        out_specs=(P("expert", "dp", None), P("expert", "dp", None), rows),
        check_vma=False,
    )
```

```python
import jax
import jax.numpy as jnp
from jax import lax
from jax.experimental import pallas as pl
from jax.experimental.pallas import tpu as pltpu
from jax.sharding import PartitionSpec as P

MESH = pl.DeviceIdType.MESH
NZ, NX, NY = 8, 4, 4
TOK = 128
CAP = 16
EXP_DEV = 4
D = 4096
FF = 768
NC = 8
DC = D // NC
UNITS = 2 * NC
ROWS = NX * CAP
SLOTS = NZ * ROWS
BLK = FF // (2 * NY)
HALF = FF // 2
AHEAD = 2
F32 = jnp.float32
BF16 = jnp.bfloat16


def kernel(
    x_hbm, dy_hbm, probs_ref, routes_ref, gate_hbm, up_hbm, w_hbm,
    down_hbm, up_out, pg_ref,
    tok, far, stg, stf, recv, part, exr, yr, wv, gatev, hid, bg, lhs, sel, meta, metar, metaf, sg1, sg1r, sg2, sg2r,
    down_ref, upo_ref, ld, od, zs, zr, xs, xr, es, er, ys, yrs, misc, cx, cy,
):
    dp = lax.axis_index("dp")
    e = lax.axis_index("expert")
    y, core = lax.div(dp, 2), lax.rem(dp, 2)
    z, x = lax.div(e, NX), lax.rem(e, NX)

    def at_z(zz):
        return (dp, lax.rem(zz, NZ) * NX + x)

    def at_x(xx):
        return (dp, z * NX + lax.rem(xx, NX))

    def at_y(yy):
        return (lax.rem(yy, NY) * 2 + core, e)

    partner = (y * 2 + 1 - core, e)

    def remote(src, dst, send, recv_sem, dev):
        return pltpu.make_async_remote_copy(
            src_ref=src, dst_ref=dst, send_sem=send, recv_sem=recv_sem,
            device_id=dev, device_id_type=MESH,
        )

    def drain(ref, sem):
        pltpu.make_async_copy(ref, ref, sem).wait()

    barrier = pltpu.get_barrier_semaphore()

    def greet(dev):
        pl.semaphore_signal(barrier, inc=1, device_id=dev, device_id_type=MESH)

    for i in range(1, NZ):
        greet(at_z(z + i))
    for i in range(1, NX):
        greet(at_x(x + i))
    for i in range(1, NY):
        greet(at_y(y + i))
    greet(partner)

    dy_loads = [
        pltpu.make_async_copy(dy_hbm.at[:, c * DC:(c + 1) * DC], tok.at[c, 0], ld.at[c])
        for c in range(NC)
    ]
    step = D // 8
    x_loads = [
        pltpu.make_async_copy(
            x_hbm.at[:, (2 * i + c % 2) * step + c // 2 * 128:(2 * i + c % 2) * step + (c // 2 + 1) * 128],
            tok.at[NC + c, 0, :, i * 128:(i + 1) * 128],
            ld.at[NC + 3],
        )
        for c in range(NC)
        for i in range(NY)
    ]
    g_load = pltpu.make_async_copy(gate_hbm, gatev, ld.at[NC])
    u_load = pltpu.make_async_copy(up_hbm, hid, ld.at[NC + 1])
    w_load = pltpu.make_async_copy(w_hbm, wv, ld.at[NC + 2])
    for c in dy_loads:
        c.start()
    g_load.start()
    u_load.start()
    for c in x_loads:
        c.start()
    w_load.start()

    def zcopy(u, src, dst, sign):
        way = sign * (1 - 2 * lax.rem(u, 2))
        return remote(tok.at[u, src], tok.at[u, dst], zs.at[lax.rem(u, NC)], zr.at[lax.rem(u, NC), dst], at_z(z + NZ + way))

    def zfar(u, src, dst, sign):
        way = sign * (1 - 2 * lax.rem(u, 2))
        i = dst - 4
        c = lax.rem(u, NC)
        s = sel[lax.div(u, NC), NZ + 2 * lax.rem(u, 2) + i]
        rows = jnp.dot(s, tok[u, src], preferred_element_type=F32).astype(BF16)
        far[c, i] = rows.reshape(NX, CAP, DC)
        remote(far.at[c, i], stf.at[u, i], zs.at[lax.rem(u, NC)], zr.at[lax.rem(u, NC), 2 + dst], at_z(z + NZ + way)).start()

    def send_own(u):
        zcopy(u, 0, 1, 1).start()
        zcopy(u, 0, 5, -1).start()

    r = routes_ref[...]
    p = probs_ref[...].astype(F32)
    owners = NZ * NX
    wid = lax.broadcasted_iota(jnp.int32, (owners, TOK), 0) * EXP_DEV
    routed = jnp.zeros((owners, TOK), F32)
    weight = jnp.zeros((owners, TOK), F32)
    for k in range(8):
        hit = wid == r[k:k + 1, :]
        routed = jnp.where(hit, 1.0, routed)
        weight = jnp.where(hit, p[k:k + 1, :], weight)
    earlier = lax.broadcasted_iota(jnp.int32, (TOK, TOK), 0) < lax.broadcasted_iota(
        jnp.int32, (TOK, TOK), 1
    )
    before = jnp.dot(
        routed.astype(BF16), jnp.where(earlier, 1.0, 0.0).astype(BF16), preferred_element_type=F32
    )
    pos = jnp.where((routed > 0.0) & (before < float(CAP)), before, -1.0)
    for i in range(NZ):
        meta[i, 0:NX, :] = pos[i * NX:(i + 1) * NX]
        meta[i, NX:2 * NX, :] = weight[i * NX:(i + 1) * NX]
    metar[z] = meta[z]

    pl.semaphore_wait(barrier, NZ + NX + NY - 2)
    for i in range(1, NZ):
        to = lax.rem(z + i, NZ)
        remote(meta.at[to], metar.at[z], misc.at[0], misc.at[1], at_z(to)).start()
    for i, (node, plane) in enumerate(((3, 4), (6, 5), (5, 4), (2, 3))):
        plane = lax.rem(z + plane, NZ)
        remote(meta.at[plane], metaf.at[i], misc.at[6], misc.at[7], at_z(z + node)).start()
    for c in range(NC):
        dy_loads[c].wait()
        if c < max(AHEAD, 1):
            send_own(c)
    g_load.wait()
    u_load.wait()

    gate = gatev[...].astype(F32)
    act = gate / (1.0 + jnp.exp(-gate))
    hidden = (act * hid[...].astype(F32)).astype(BF16)
    hid[...] = hidden
    lhs[0] = hidden.T
    bg[...] = jnp.zeros_like(bg)
    drain(x_hbm, ld.at[NC + 3])
    w_load.wait()

    drain(metar.at[0:NZ - 1], misc.at[1])
    drain(metaf, misc.at[7])
    slot_pos = lax.broadcasted_iota(jnp.int32, (NX, CAP, TOK), 1).astype(F32)

    def build(m, i):
        at = m[0:NX].reshape(NX, 1, TOK)
        wt = m[NX:2 * NX].reshape(NX, 1, TOK)
        hit = jnp.broadcast_to(at, (NX, CAP, TOK)) == slot_pos
        one = jnp.where(hit, 1.0, 0.0)
        wtd = jnp.where(hit, jnp.broadcast_to(wt, (NX, CAP, TOK)), 0.0)
        sel[0, i] = wtd.reshape(ROWS, TOK).astype(BF16)
        sel[1, i] = one.reshape(ROWS, TOK).astype(BF16)

    for i in range(NZ):
        build(metar[i], i)
    for i in range(4):
        build(metaf[i], NZ + i)

    def pick(u, j):
        way = 1 - 2 * lax.rem(u, 2)
        src = lax.rem(z + 8 * NZ - way * j, NZ)
        c = lax.rem(u, NC)
        i = j if j < 4 else j - 2
        s = sel[lax.div(u, NC), src]
        rows = jnp.dot(s, tok[u, i], preferred_element_type=F32).astype(BF16)
        stg[c, i] = rows.reshape(NX, CAP, DC)
        spread(u, j, stg.at[c, i])

    def spread(u, j, ref):
        way = 1 - 2 * lax.rem(u, 2)
        src = lax.rem(z + 8 * NZ - way * j, NZ)
        slot = src * NX + x
        recv[u, slot] = ref[x]
        for i in range(1, NX):
            to = lax.rem(x + i, NX)
            remote(ref.at[to], recv.at[u, slot], xs.at[lax.rem(u, NC)], xr.at[lax.rem(u, NC)], at_x(to)).start()

    def on(k, t, body):
        u = k - t

        @pl.when((u >= 0) & (u < UNITS))
        def _():
            body(u)

    def relay1(u):
        drain(tok.at[u, 1], zr.at[lax.rem(u, NC), 1])
        zcopy(u, 1, 2, 1).start()
        drain(tok.at[u, 5], zr.at[lax.rem(u, NC), 5])
        zcopy(u, 5, 4, -1).start()

    def relay2(u):
        drain(tok.at[u, 2], zr.at[lax.rem(u, NC), 2])
        zcopy(u, 2, 3, 1).start()
        drain(tok.at[u, 4], zr.at[lax.rem(u, NC), 4])
        zfar(u, 4, 5, -1)

    def relay3(u):
        drain(tok.at[u, 3], zr.at[lax.rem(u, NC), 3])
        zfar(u, 3, 4, 1)

    def pick1(u):
        pick(u, 0)
        pick(u, 1)
        pick(u, 7)

    def pick2(u):
        pick(u, 2)
        pick(u, 6)

    def pick3(u):
        pick(u, 3)
        drain(stf.at[u, 1], zr.at[lax.rem(u, NC), 7])
        spread(u, 5, stf.at[u, 1])

    def pick4(u):
        drain(stf.at[u, 0], zr.at[lax.rem(u, NC), 6])
        spread(u, 4, stf.at[u, 0])

    def compute(u):
        c = lax.rem(u, NC)
        kind = lax.div(u, NC)
        drain(recv.at[u, 0:NZ * (NX - 1)], xr.at[lax.rem(u, NC)])

        @pl.when(kind == 0)
        def _():
            a = recv[u].reshape(SLOTS, DC)
            wc = wv[:, pl.ds(pl.multiple_of(c * DC, DC), DC)]
            bg[...] += lax.dot_general(
                a, wc, (((1,), (1,)), ((), ())), preferred_element_type=F32
            )

        def tile(n, carry):
            cols = recv[u, :, :, pl.ds(pl.multiple_of(n * 256, 256), 256)].reshape(SLOTS, 256)
            prod = jnp.dot(lhs[kind], cols, preferred_element_type=F32).astype(BF16)

            @pl.when(kind == 0)
            def _():
                for d in range(2 * NY):
                    for h in range(2):
                        part[c, d % 2 * NY + d // 2, pl.ds(pl.multiple_of((2 * n + h) * BLK, BLK), BLK), :] = (
                            prod[d * BLK:(d + 1) * BLK, h * 128:(h + 1) * 128]
                        )

            @pl.when(kind == 1)
            def _():
                for i in range(2):
                    for h in range(2):
                        part[c, 4 * n + 2 * i + h] = (
                            prod[h * HALF:(h + 1) * HALF, i * 128:(i + 1) * 128]
                        )

                @pl.when(core != lax.rem(c, 2))
                def _():
                    for i in range(2):
                        m = 2 * n + i
                        ref = pl.ds(2 * m, 2)
                        remote(part.at[c, ref], exr.at[c, ref], es.at[lax.rem(u, NC)], er.at[lax.rem(u, NC), m], partner).start()

            return carry

        @pl.when(kind == 1)
        def _():
            pl.semaphore_wait(cx.at[c], 1)

        lax.fori_loop(0, DC // 256, tile, 0)

        @pl.when(kind == 0)
        def _():
            for m in range(NY):
                remote(
                    part.at[c, (1 - core) * NY + m], exr.at[c, m], es.at[lax.rem(u, NC)], er.at[lax.rem(u, NC), m], partner
                ).start()

        @pl.when(u == NC - 1)
        def _():
            back = bg[...]
            g = gatev[...].astype(F32)
            pre = (back * (g / (1.0 + jnp.exp(-g)))).astype(BF16)
            lhs[1] = pre.T
            sg = jnp.sum(hid[...].astype(F32) * back, axis=1, keepdims=True)
            lane = lax.broadcasted_iota(jnp.int32, (SLOTS, TOK), 1)
            row = lax.broadcasted_iota(jnp.int32, (SLOTS, TOK), 0)
            spread = jnp.where(lane == x * CAP + lax.rem(row, CAP), sg, 0.0)
            packed = jnp.sum(spread.reshape(NZ * NX, CAP, TOK), axis=1)
            for s in range(NZ * NX):
                sg1[s % NX, s // NX:s // NX + 1, :] = packed[s:s + 1, :]
            sg1r[x] = sg1[x]
            for i in range(1, NX):
                to = lax.rem(x + i, NX)
                remote(sg1.at[to], sg1r.at[x], misc.at[2], misc.at[3], at_x(to)).start()

    def chip_sum(u):
        c = lax.rem(u, NC)
        drain(tok.at[u, 0:6], zs.at[lax.rem(u, NC)])
        drain(recv.at[u, 0:NZ * (NX - 1)], xs.at[lax.rem(u, NC)])

        @pl.when(u < NC)
        def _():
            for i in (2, 3, 1):
                to = lax.rem(y + i, NY)
                mine = core * NY + to
                drain(exr.at[c, to], er.at[lax.rem(u, NC), to])
                part[c, mine] = (part[c, mine].astype(F32) + exr[c, to].astype(F32)).astype(BF16)
                remote(part.at[c, mine], yr.at[c, i - 1, 0], ys.at[lax.rem(u, NC)], yrs.at[lax.rem(u, NC)], at_y(to)).start()

        @pl.when(u >= NC)
        def _():
            pl.semaphore_wait(cy.at[c], NY - 1)

        @pl.when((u >= NC) & (core == lax.rem(c, 2)))
        def _():
            for i in (2, 3, 1):
                to = lax.rem(y + i, NY)
                ref = pl.ds(2 * to, 2)
                drain(exr.at[c, ref], er.at[lax.rem(u, NC), to])
                for h in range(2):
                    m = 2 * to + h
                    part[c, m] = (part[c, m].astype(F32) + exr[c, m].astype(F32)).astype(BF16)
                remote(part.at[c, ref], yr.at[c, i - 1], ys.at[lax.rem(u, NC)], yrs.at[lax.rem(u, NC)], at_y(to)).start()

    def finish_down(u):
        c = u
        drain(exr.at[c, y], er.at[lax.rem(u, NC), y])
        drain(part.at[c, 0:NY - 1], yrs.at[lax.rem(u, NC)])
        total = part[c, core * NY + y].astype(F32) + exr[c, y].astype(F32)
        for i in range(NY - 1):
            total = total + yr[c, i, 0].astype(F32)
        for i in range(DC // 128):
            down_ref[:, pl.ds(pl.multiple_of(c * DC + i * 128, 128), 128)] = (
                total[i * BLK:(i + 1) * BLK]
            )
        cols = pl.ds(pl.multiple_of(c * DC, DC), DC)
        pltpu.make_async_copy(down_ref.at[:, cols], down_hbm.at[:, cols], od.at[0]).start()
        pl.semaphore_signal(cx.at[c], inc=1, device_id=partner, device_id_type=MESH)
        for i in range(1, NY):
            pl.semaphore_signal(cy.at[c], inc=1, device_id=at_y(y + i), device_id_type=MESH)
        drain(part.at[c, 0:NY], es.at[lax.rem(u, NC)])
        drain(part.at[c, 0:NY - 1], ys.at[lax.rem(u, NC)])

    def finish_up(u):
        c = lax.rem(u, NC)
        own = core == lax.rem(c, 2)

        @pl.when(own)
        def _():
            drain(exr.at[c, pl.ds(2 * y, 2)], er.at[lax.rem(u, NC), y])
            drain(yr.at[c], yrs.at[lax.rem(u, NC)])
            for h in range(2):
                total = part[c, 2 * y + h].astype(F32) + exr[c, 2 * y + h].astype(F32)
                for i in range(NY - 1):
                    total = total + yr[c, i, h].astype(F32)
                upo_ref[
                    pl.ds(pl.multiple_of(lax.div(c, 2) * 128, 128), 128), h * HALF:(h + 1) * HALF
                ] = total.T.astype(BF16)
            out = pl.ds(pl.multiple_of(lax.div(c, 2) * 128, 128), 128)
            pltpu.make_async_copy(upo_ref.at[out], up_out.at[out], od.at[1]).start()
            drain(yr.at[c], ys.at[lax.rem(u, NC)])

        @pl.when(jnp.logical_not(own))
        def _():
            drain(part.at[c], es.at[lax.rem(u, NC)])

    def grads_over_z():
        drain(sg1r.at[0:NX - 1], misc.at[3])
        both = sg1r[0] + sg1r[1] + sg1r[2] + sg1r[3]
        for i in range(NZ):
            sg2[i] = jnp.broadcast_to(both[i:i + 1, :], (8, TOK))
        sg2r[z] = sg2[z]
        for i in range(1, NZ):
            to = lax.rem(z + i, NZ)
            remote(sg2.at[to], sg2r.at[z], misc.at[4], misc.at[5], at_z(to)).start()

    def grads_out():
        drain(sg2r.at[0:NZ - 1], misc.at[5])
        eye = lax.broadcasted_iota(jnp.int32, (TOK, TOK), 0) == lax.broadcasted_iota(
            jnp.int32, (TOK, TOK), 1
        )
        rr = routes_ref[...]
        total = jnp.zeros((8, TOK), F32)
        for i in range(NZ):
            spread = jnp.where(eye, jnp.broadcast_to(sg2r[i, 0:1, :], (TOK, TOK)), 0.0)
            column = jnp.sum(spread, axis=1, keepdims=True)[0:ROWS].reshape(NX, CAP, 1)
            at = meta[i, 0:NX, :].reshape(NX, 1, TOK)
            hit = jnp.broadcast_to(at, (NX, CAP, TOK)) == slot_pos
            got = jnp.sum(jnp.where(hit, column, 0.0), axis=1)
            for j in range(NX):
                total = jnp.where(rr == (i * NX + j) * EXP_DEV, got[j:j + 1, :], total)
        pg_ref[...] = total / probs_ref[...].astype(F32)
        drain(meta.at[0:NZ - 1], misc.at[0])
        drain(metaf, misc.at[6])
        drain(sg1.at[0:NX - 1], misc.at[2])
        drain(sg2.at[0:NZ - 1], misc.at[4])

    def body(k, carry):
        on(k, 0, relay1)
        on(k, 4, chip_sum)
        on(k, 1, relay3)

        @pl.when(k + AHEAD < UNITS)
        def _():
            send_own(k + AHEAD)

        on(k, 0, pick1)
        on(k, 1, pick3)
        on(k, 2, pick4)
        on(k, 3, compute)

        @pl.when((k >= 6) & (k < NC + 6))
        def _():
            finish_down(k - 6)

        @pl.when(k == NC + 3)
        def _():
            grads_over_z()

        @pl.when(k == NC + 5)
        def _():
            grads_out()

        on(k, 0, relay2)
        on(k, 0, pick2)
        return carry

    lax.fori_loop(0, UNITS + 4, body, 0)

    def last(u, carry):
        finish_up(u)
        return carry

    lax.fori_loop(NC, UNITS, last, 0)
    drain(down_ref, od.at[0])
    drain(upo_ref, od.at[1])


def per_device(tokens, out_grad, probs, routes, saved_gate, saved_up, down_weight):
    anyspace = pl.BlockSpec(memory_space=pl.ANY)
    vmem = pl.BlockSpec(memory_space=pltpu.VMEM)
    dma = pltpu.SemaphoreType.DMA
    down, up, pg = pl.pallas_call(
        kernel,
        out_shape=(
            jax.ShapeDtypeStruct((BLK, D), F32),
            jax.ShapeDtypeStruct((D // 8, FF), BF16),
            jax.ShapeDtypeStruct((8, TOK), F32),
        ),
        in_specs=[anyspace, anyspace, vmem, vmem, anyspace, anyspace, anyspace],
        out_specs=(anyspace, anyspace, vmem),
        scratch_shapes=[
            pltpu.VMEM((UNITS, 6, TOK, DC), BF16),
            pltpu.VMEM((NC, 2, NX, CAP, DC), BF16),
            pltpu.VMEM((NC, 6, NX, CAP, DC), BF16),
            pltpu.VMEM((UNITS, 2, NX, CAP, DC), BF16),
            pltpu.VMEM((UNITS, NZ * NX, CAP, DC), BF16),
            pltpu.VMEM((NC, 2 * NY, HALF, 128), BF16),
            pltpu.VMEM((NC, 2 * NY, HALF, 128), BF16),
            pltpu.VMEM((NC, NY - 1, 2, HALF, 128), BF16),
            pltpu.VMEM((FF, D), BF16),
            pltpu.VMEM((SLOTS, FF), BF16),
            pltpu.VMEM((SLOTS, FF), BF16),
            pltpu.VMEM((SLOTS, FF), F32),
            pltpu.VMEM((2, FF, SLOTS), BF16),
            pltpu.VMEM((2, NZ + 4, ROWS, TOK), BF16),
            pltpu.VMEM((NZ, 8, TOK), F32),
            pltpu.VMEM((NZ, 8, TOK), F32),
            pltpu.VMEM((4, 8, TOK), F32),
            pltpu.VMEM((NX, NZ, TOK), F32),
            pltpu.VMEM((NX, NZ, TOK), F32),
            pltpu.VMEM((NZ, 8, TOK), F32),
            pltpu.VMEM((NZ, 8, TOK), F32),
            pltpu.VMEM((BLK, D), F32),
            pltpu.VMEM((D // 8, FF), BF16),
            dma((NC + 4,)),
            dma((2,)),
            dma((NC,)),
            dma((NC, NZ)),
            dma((NC,)),
            dma((NC,)),
            dma((NC,)),
            dma((NC, NY)),
            dma((NC,)),
            dma((NC,)),
            dma((8,)),
            pltpu.SemaphoreType.REGULAR((NC,)),
            pltpu.SemaphoreType.REGULAR((NC,)),
        ],
        compiler_params=pltpu.CompilerParams(
            collective_id=0, has_side_effects=True, vmem_limit_bytes=67043328
        ),
        name="expert_grads",
    )(
        tokens, out_grad, probs.T, routes.T, saved_gate, saved_up,
        down_weight.reshape(down_weight.shape[1:]),
    )
    return down[None], up[None], pg.T


def solution(mesh):
    rows = P(("dp", "expert"), None)
    return jax.shard_map(
        per_device,
        mesh=mesh,
        in_specs=(rows, rows, rows, rows, rows, rows, P("expert", None, None)),
        out_specs=(P("expert", "dp", None), P("expert", "dp", None), rows),
        check_vma=False,
    )
```

```python
import jax
import jax.numpy as jnp
from jax import lax
from jax.experimental import pallas as pl
from jax.experimental.pallas import tpu as pltpu
from jax.sharding import PartitionSpec as P

MESH = pl.DeviceIdType.MESH
NZ, NX, NY = 8, 4, 4
TOK = 128
CAP = 16
EXP_DEV = 4
D = 4096
FF = 768
NC = 8
DC = D // NC
UNITS = 2 * NC
ROWS = NX * CAP
SLOTS = NZ * ROWS
BLK = FF // (2 * NY)
HALF = FF // 2
AHEAD = 2
F32 = jnp.float32
BF16 = jnp.bfloat16


def kernel(
    x_hbm, dy_hbm, probs_ref, routes_ref, gate_hbm, up_hbm, w_hbm,
    down_hbm, up_out, pg_ref,
    tok, far, stg, stf, recv, part, exr, yr, wv, gatev, hid, bg, lhs, sel, meta, metar, metaf, sg1, sg1r, sg2, sg2r,
    down_ref, upo_ref, ld, od, zs, zr, xs, xr, es, er, ys, yrs, misc, cx, cy,
):
    dp = lax.axis_index("dp")
    e = lax.axis_index("expert")
    y, core = lax.div(dp, 2), lax.rem(dp, 2)
    z, x = lax.div(e, NX), lax.rem(e, NX)

    def at_z(zz):
        return (dp, lax.rem(zz, NZ) * NX + x)

    def at_x(xx):
        return (dp, z * NX + lax.rem(xx, NX))

    def at_y(yy):
        return (lax.rem(yy, NY) * 2 + core, e)

    partner = (y * 2 + 1 - core, e)

    def remote(src, dst, send, recv_sem, dev):
        return pltpu.make_async_remote_copy(
            src_ref=src, dst_ref=dst, send_sem=send, recv_sem=recv_sem,
            device_id=dev, device_id_type=MESH,
        )

    def drain(ref, sem):
        pltpu.make_async_copy(ref, ref, sem).wait()

    barrier = pltpu.get_barrier_semaphore()

    def greet(dev):
        pl.semaphore_signal(barrier, inc=1, device_id=dev, device_id_type=MESH)

    for i in range(1, NZ):
        greet(at_z(z + i))
    for i in range(1, NX):
        greet(at_x(x + i))
    for i in range(1, NY):
        greet(at_y(y + i))
    greet(partner)

    dy_loads = [
        pltpu.make_async_copy(dy_hbm.at[:, c * DC:(c + 1) * DC], tok.at[c, 0], ld.at[c])
        for c in range(NC)
    ]
    step = D // 8
    x_loads = [
        pltpu.make_async_copy(
            x_hbm.at[:, (2 * i + c % 2) * step + c // 2 * 128:(2 * i + c % 2) * step + (c // 2 + 1) * 128],
            tok.at[NC + c, 0, :, i * 128:(i + 1) * 128],
            ld.at[NC + 3],
        )
        for c in range(NC)
        for i in range(NY)
    ]
    g_load = pltpu.make_async_copy(gate_hbm, gatev, ld.at[NC])
    u_load = pltpu.make_async_copy(up_hbm, hid, ld.at[NC + 1])
    w_load = pltpu.make_async_copy(w_hbm, wv, ld.at[NC + 2])
    for c in dy_loads:
        c.start()
    g_load.start()
    u_load.start()
    for c in x_loads:
        c.start()
    w_load.start()

    def zcopy(u, src, dst, sign):
        way = sign * (1 - 2 * lax.rem(u, 2))
        return remote(tok.at[u, src], tok.at[u, dst], zs.at[lax.rem(u, NC)], zr.at[lax.rem(u, NC), dst], at_z(z + NZ + way))

    def zfar(u, src, dst, sign):
        way = sign * (1 - 2 * lax.rem(u, 2))
        i = dst - 4
        c = lax.rem(u, NC)
        s = sel[lax.div(u, NC), NZ + 2 * lax.rem(u, 2) + i]
        rows = jnp.dot(s, tok[u, src], preferred_element_type=F32).astype(BF16)
        far[c, i] = rows.reshape(NX, CAP, DC)
        remote(far.at[c, i], stf.at[u, i], zs.at[lax.rem(u, NC)], zr.at[lax.rem(u, NC), 2 + dst], at_z(z + NZ + way)).start()

    def send_own(u):
        zcopy(u, 0, 1, 1).start()
        zcopy(u, 0, 5, -1).start()

    r = routes_ref[...]
    p = probs_ref[...].astype(F32)
    owners = NZ * NX
    wid = lax.broadcasted_iota(jnp.int32, (owners, TOK), 0) * EXP_DEV
    routed = jnp.zeros((owners, TOK), F32)
    weight = jnp.zeros((owners, TOK), F32)
    for k in range(8):
        hit = wid == r[k:k + 1, :]
        routed = jnp.where(hit, 1.0, routed)
        weight = jnp.where(hit, p[k:k + 1, :], weight)
    earlier = lax.broadcasted_iota(jnp.int32, (TOK, TOK), 0) < lax.broadcasted_iota(
        jnp.int32, (TOK, TOK), 1
    )
    before = jnp.dot(
        routed.astype(BF16), jnp.where(earlier, 1.0, 0.0).astype(BF16), preferred_element_type=F32
    )
    pos = jnp.where((routed > 0.0) & (before < float(CAP)), before, -1.0)
    for i in range(NZ):
        meta[i, 0:NX, :] = pos[i * NX:(i + 1) * NX]
        meta[i, NX:2 * NX, :] = weight[i * NX:(i + 1) * NX]
    metar[z] = meta[z]

    pl.semaphore_wait(barrier, NZ + NX + NY - 2)
    for i in range(1, NZ):
        to = lax.rem(z + i, NZ)
        remote(meta.at[to], metar.at[z], misc.at[0], misc.at[1], at_z(to)).start()
    for i, (node, plane) in enumerate(((3, 4), (6, 5), (5, 4), (2, 3))):
        plane = lax.rem(z + plane, NZ)
        remote(meta.at[plane], metaf.at[i], misc.at[6], misc.at[7], at_z(z + node)).start()
    for c in range(NC):
        dy_loads[c].wait()
        if c < max(AHEAD, 1):
            send_own(c)
    g_load.wait()
    u_load.wait()

    gate = gatev[...].astype(F32)
    act = gate / (1.0 + jnp.exp(-gate))
    hidden = (act * hid[...].astype(F32)).astype(BF16)
    hid[...] = hidden
    lhs[0] = hidden.T
    bg[...] = jnp.zeros_like(bg)
    drain(x_hbm, ld.at[NC + 3])
    w_load.wait()

    drain(metar.at[0:NZ - 1], misc.at[1])
    drain(metaf, misc.at[7])
    slot_pos = lax.broadcasted_iota(jnp.int32, (NX, CAP, TOK), 1).astype(F32)

    def build(m, i):
        at = m[0:NX].reshape(NX, 1, TOK)
        wt = m[NX:2 * NX].reshape(NX, 1, TOK)
        hit = jnp.broadcast_to(at, (NX, CAP, TOK)) == slot_pos
        one = jnp.where(hit, 1.0, 0.0)
        wtd = jnp.where(hit, jnp.broadcast_to(wt, (NX, CAP, TOK)), 0.0)
        sel[0, i] = wtd.reshape(ROWS, TOK).astype(BF16)
        sel[1, i] = one.reshape(ROWS, TOK).astype(BF16)

    for i in range(NZ):
        build(metar[i], i)
    for i in range(4):
        build(metaf[i], NZ + i)

    def pick(u, j):
        way = 1 - 2 * lax.rem(u, 2)
        src = lax.rem(z + 8 * NZ - way * j, NZ)
        c = lax.rem(u, NC)
        i = j if j < 4 else j - 2
        s = sel[lax.div(u, NC), src]
        rows = jnp.dot(s, tok[u, i], preferred_element_type=F32).astype(BF16)
        stg[c, i] = rows.reshape(NX, CAP, DC)
        spread(u, j, stg.at[c, i])

    def spread(u, j, ref):
        way = 1 - 2 * lax.rem(u, 2)
        src = lax.rem(z + 8 * NZ - way * j, NZ)
        slot = src * NX + x
        recv[u, slot] = ref[x]
        for i in range(1, NX):
            to = lax.rem(x + i, NX)
            remote(ref.at[to], recv.at[u, slot], xs.at[lax.rem(u, NC)], xr.at[lax.rem(u, NC)], at_x(to)).start()

    def on(k, t, body):
        u = k - t

        @pl.when((u >= 0) & (u < UNITS))
        def _():
            body(u)

    def relay1(u):
        drain(tok.at[u, 1], zr.at[lax.rem(u, NC), 1])
        zcopy(u, 1, 2, 1).start()
        drain(tok.at[u, 5], zr.at[lax.rem(u, NC), 5])
        zcopy(u, 5, 4, -1).start()

    def relay2(u):
        drain(tok.at[u, 2], zr.at[lax.rem(u, NC), 2])
        zcopy(u, 2, 3, 1).start()
        drain(tok.at[u, 4], zr.at[lax.rem(u, NC), 4])
        zfar(u, 4, 5, -1)

    def relay3(u):
        drain(tok.at[u, 3], zr.at[lax.rem(u, NC), 3])
        zfar(u, 3, 4, 1)

    def pick1(u):
        pick(u, 0)
        pick(u, 1)
        pick(u, 7)

    def pick2(u):
        pick(u, 2)
        pick(u, 6)

    def pick3(u):
        pick(u, 3)
        drain(stf.at[u, 1], zr.at[lax.rem(u, NC), 7])
        spread(u, 5, stf.at[u, 1])

    def pick4(u):
        drain(stf.at[u, 0], zr.at[lax.rem(u, NC), 6])
        spread(u, 4, stf.at[u, 0])

    def compute(u):
        c = lax.rem(u, NC)
        kind = lax.div(u, NC)
        drain(recv.at[u, 0:NZ * (NX - 1)], xr.at[lax.rem(u, NC)])

        @pl.when(kind == 0)
        def _():
            a = recv[u].reshape(SLOTS, DC)
            wc = wv[:, pl.ds(pl.multiple_of(c * DC, DC), DC)]
            bg[...] += lax.dot_general(
                a, wc, (((1,), (1,)), ((), ())), preferred_element_type=F32
            )

        def tile(n, carry):
            cols = recv[u, :, :, pl.ds(pl.multiple_of(n * 256, 256), 256)].reshape(SLOTS, 256)
            prod = jnp.dot(lhs[kind], cols, preferred_element_type=F32).astype(BF16)

            @pl.when(kind == 0)
            def _():
                for d in range(2 * NY):
                    for h in range(2):
                        part[c, d % 2 * NY + d // 2, pl.ds(pl.multiple_of((2 * n + h) * BLK, BLK), BLK), :] = (
                            prod[d * BLK:(d + 1) * BLK, h * 128:(h + 1) * 128]
                        )

            @pl.when(kind == 1)
            def _():
                for i in range(2):
                    for h in range(2):
                        part[c, 4 * n + 2 * i + h] = (
                            prod[h * HALF:(h + 1) * HALF, i * 128:(i + 1) * 128]
                        )

                @pl.when(core != lax.rem(c, 2))
                def _():
                    for i in range(2):
                        m = 2 * n + i
                        ref = pl.ds(2 * m, 2)
                        remote(part.at[c, ref], exr.at[c, ref], es.at[lax.rem(u, NC)], er.at[lax.rem(u, NC), m], partner).start()

            return carry

        @pl.when(kind == 1)
        def _():
            pl.semaphore_wait(cx.at[c], 1)

        lax.fori_loop(0, DC // 256, tile, 0)

        @pl.when(kind == 0)
        def _():
            for m in range(NY):
                remote(
                    part.at[c, (1 - core) * NY + m], exr.at[c, m], es.at[lax.rem(u, NC)], er.at[lax.rem(u, NC), m], partner
                ).start()

        @pl.when(u == NC - 1)
        def _():
            back = bg[...]
            g = gatev[...].astype(F32)
            pre = (back * (g / (1.0 + jnp.exp(-g)))).astype(BF16)
            lhs[1] = pre.T
            sg = jnp.sum(hid[...].astype(F32) * back, axis=1, keepdims=True)
            lane = lax.broadcasted_iota(jnp.int32, (SLOTS, TOK), 1)
            row = lax.broadcasted_iota(jnp.int32, (SLOTS, TOK), 0)
            spread = jnp.where(lane == x * CAP + lax.rem(row, CAP), sg, 0.0)
            packed = jnp.sum(spread.reshape(NZ * NX, CAP, TOK), axis=1)
            for s in range(NZ * NX):
                sg1[s % NX, s // NX:s // NX + 1, :] = packed[s:s + 1, :]
            sg1r[x] = sg1[x]
            for i in range(1, NX):
                to = lax.rem(x + i, NX)
                remote(sg1.at[to], sg1r.at[x], misc.at[2], misc.at[3], at_x(to)).start()

    def chip_sum(u):
        c = lax.rem(u, NC)
        drain(tok.at[u, 0:6], zs.at[lax.rem(u, NC)])
        drain(recv.at[u, 0:NZ * (NX - 1)], xs.at[lax.rem(u, NC)])

        @pl.when(u < NC)
        def _():
            for i in (2, 3, 1):
                to = lax.rem(y + i, NY)
                mine = core * NY + to
                drain(exr.at[c, to], er.at[lax.rem(u, NC), to])
                part[c, mine] = (part[c, mine].astype(F32) + exr[c, to].astype(F32)).astype(BF16)
                remote(part.at[c, mine], yr.at[c, i - 1, 0], ys.at[lax.rem(u, NC)], yrs.at[lax.rem(u, NC)], at_y(to)).start()

        @pl.when(u >= NC)
        def _():
            pl.semaphore_wait(cy.at[c], NY - 1)

        @pl.when((u >= NC) & (core == lax.rem(c, 2)))
        def _():
            for i in (2, 3, 1):
                to = lax.rem(y + i, NY)
                ref = pl.ds(2 * to, 2)
                drain(exr.at[c, ref], er.at[lax.rem(u, NC), to])
                for h in range(2):
                    m = 2 * to + h
                    part[c, m] = (part[c, m].astype(F32) + exr[c, m].astype(F32)).astype(BF16)
                remote(part.at[c, ref], yr.at[c, i - 1], ys.at[lax.rem(u, NC)], yrs.at[lax.rem(u, NC)], at_y(to)).start()

    def finish_down(u):
        c = u
        drain(exr.at[c, y], er.at[lax.rem(u, NC), y])
        drain(part.at[c, 0:NY - 1], yrs.at[lax.rem(u, NC)])
        total = part[c, core * NY + y].astype(F32) + exr[c, y].astype(F32)
        for i in range(NY - 1):
            total = total + yr[c, i, 0].astype(F32)
        for i in range(DC // 128):
            down_ref[:, pl.ds(pl.multiple_of(c * DC + i * 128, 128), 128)] = (
                total[i * BLK:(i + 1) * BLK]
            )
        cols = pl.ds(pl.multiple_of(c * DC, DC), DC)
        pltpu.make_async_copy(down_ref.at[:, cols], down_hbm.at[:, cols], od.at[0]).start()
        pl.semaphore_signal(cx.at[c], inc=1, device_id=partner, device_id_type=MESH)
        for i in range(1, NY):
            pl.semaphore_signal(cy.at[c], inc=1, device_id=at_y(y + i), device_id_type=MESH)
        drain(part.at[c, 0:NY], es.at[lax.rem(u, NC)])
        drain(part.at[c, 0:NY - 1], ys.at[lax.rem(u, NC)])

    def finish_up(u):
        c = lax.rem(u, NC)
        own = core == lax.rem(c, 2)

        @pl.when(own)
        def _():
            drain(exr.at[c, pl.ds(2 * y, 2)], er.at[lax.rem(u, NC), y])
            drain(yr.at[c], yrs.at[lax.rem(u, NC)])
            for h in range(2):
                total = part[c, 2 * y + h].astype(F32) + exr[c, 2 * y + h].astype(F32)
                for i in range(NY - 1):
                    total = total + yr[c, i, h].astype(F32)
                upo_ref[
                    pl.ds(pl.multiple_of(lax.div(c, 2) * 128, 128), 128), h * HALF:(h + 1) * HALF
                ] = total.T.astype(BF16)
            out = pl.ds(pl.multiple_of(lax.div(c, 2) * 128, 128), 128)
            pltpu.make_async_copy(upo_ref.at[out], up_out.at[out], od.at[1]).start()
            drain(yr.at[c], ys.at[lax.rem(u, NC)])

        @pl.when(jnp.logical_not(own))
        def _():
            drain(part.at[c], es.at[lax.rem(u, NC)])

    def grads_over_z():
        drain(sg1r.at[0:NX - 1], misc.at[3])
        both = sg1r[0] + sg1r[1] + sg1r[2] + sg1r[3]
        for i in range(NZ):
            sg2[i] = jnp.broadcast_to(both[i:i + 1, :], (8, TOK))
        sg2r[z] = sg2[z]
        for i in range(1, NZ):
            to = lax.rem(z + i, NZ)
            remote(sg2.at[to], sg2r.at[z], misc.at[4], misc.at[5], at_z(to)).start()

    def grads_out():
        drain(sg2r.at[0:NZ - 1], misc.at[5])
        eye = lax.broadcasted_iota(jnp.int32, (TOK, TOK), 0) == lax.broadcasted_iota(
            jnp.int32, (TOK, TOK), 1
        )
        rr = routes_ref[...]
        total = jnp.zeros((8, TOK), F32)
        for i in range(NZ):
            spread = jnp.where(eye, jnp.broadcast_to(sg2r[i, 0:1, :], (TOK, TOK)), 0.0)
            column = jnp.sum(spread, axis=1, keepdims=True)[0:ROWS].reshape(NX, CAP, 1)
            at = meta[i, 0:NX, :].reshape(NX, 1, TOK)
            hit = jnp.broadcast_to(at, (NX, CAP, TOK)) == slot_pos
            got = jnp.sum(jnp.where(hit, column, 0.0), axis=1)
            for j in range(NX):
                total = jnp.where(rr == (i * NX + j) * EXP_DEV, got[j:j + 1, :], total)
        pg_ref[...] = total / probs_ref[...].astype(F32)
        drain(meta.at[0:NZ - 1], misc.at[0])
        drain(metaf, misc.at[6])
        drain(sg1.at[0:NX - 1], misc.at[2])
        drain(sg2.at[0:NZ - 1], misc.at[4])

    def body(k, carry):
        on(k, 0, relay1)
        on(k, 4, chip_sum)
        on(k, 1, relay3)

        @pl.when(k + AHEAD < UNITS)
        def _():
            send_own(k + AHEAD)

        on(k, 0, pick1)
        on(k, 1, pick3)
        on(k, 2, pick4)
        on(k, 3, compute)

        @pl.when((k >= 6) & (k < NC + 6))
        def _():
            finish_down(k - 6)

        @pl.when(k == NC + 3)
        def _():
            grads_over_z()

        @pl.when(k == NC + 5)
        def _():
            grads_out()

        on(k, 0, relay2)
        on(k, 0, pick2)
        return carry

    lax.fori_loop(0, UNITS + 4, body, 0)

    def last(u, carry):
        finish_up(u)
        return carry

    lax.fori_loop(NC, UNITS, last, 0)
    drain(down_ref, od.at[0])
    drain(upo_ref, od.at[1])


def hand_over(down_ref, up_ref, pg_ref, down_out, up_out, pg_out):
    down_out[...] = down_ref[...]
    up_out[...] = up_ref[...]
    pg_out[...] = pg_ref[...]


def per_device(tokens, out_grad, probs, routes, saved_gate, saved_up, down_weight):
    anyspace = pl.BlockSpec(memory_space=pl.ANY)
    vmem = pl.BlockSpec(memory_space=pltpu.VMEM)
    dma = pltpu.SemaphoreType.DMA
    down, up, pg = pl.pallas_call(
        kernel,
        out_shape=(
            jax.ShapeDtypeStruct((BLK, D), F32),
            jax.ShapeDtypeStruct((D // 8, FF), BF16),
            jax.ShapeDtypeStruct((8, TOK), F32),
        ),
        in_specs=[anyspace, anyspace, vmem, vmem, anyspace, anyspace, anyspace],
        out_specs=(anyspace, anyspace, vmem),
        scratch_shapes=[
            pltpu.VMEM((UNITS, 6, TOK, DC), BF16),
            pltpu.VMEM((NC, 2, NX, CAP, DC), BF16),
            pltpu.VMEM((NC, 6, NX, CAP, DC), BF16),
            pltpu.VMEM((UNITS, 2, NX, CAP, DC), BF16),
            pltpu.VMEM((UNITS, NZ * NX, CAP, DC), BF16),
            pltpu.VMEM((NC, 2 * NY, HALF, 128), BF16),
            pltpu.VMEM((NC, 2 * NY, HALF, 128), BF16),
            pltpu.VMEM((NC, NY - 1, 2, HALF, 128), BF16),
            pltpu.VMEM((FF, D), BF16),
            pltpu.VMEM((SLOTS, FF), BF16),
            pltpu.VMEM((SLOTS, FF), BF16),
            pltpu.VMEM((SLOTS, FF), F32),
            pltpu.VMEM((2, FF, SLOTS), BF16),
            pltpu.VMEM((2, NZ + 4, ROWS, TOK), BF16),
            pltpu.VMEM((NZ, 8, TOK), F32),
            pltpu.VMEM((NZ, 8, TOK), F32),
            pltpu.VMEM((4, 8, TOK), F32),
            pltpu.VMEM((NX, NZ, TOK), F32),
            pltpu.VMEM((NX, NZ, TOK), F32),
            pltpu.VMEM((NZ, 8, TOK), F32),
            pltpu.VMEM((NZ, 8, TOK), F32),
            pltpu.VMEM((BLK, D), F32),
            pltpu.VMEM((D // 8, FF), BF16),
            dma((NC + 4,)),
            dma((2,)),
            dma((NC,)),
            dma((NC, NZ)),
            dma((NC,)),
            dma((NC,)),
            dma((NC,)),
            dma((NC, NY)),
            dma((NC,)),
            dma((NC,)),
            dma((8,)),
            pltpu.SemaphoreType.REGULAR((NC,)),
            pltpu.SemaphoreType.REGULAR((NC,)),
        ],
        compiler_params=pltpu.CompilerParams(
            collective_id=0, has_side_effects=True, vmem_limit_bytes=67043328
        ),
        name="expert_grads",
    )(
        tokens, out_grad, probs.T, routes.T, saved_gate, saved_up,
        down_weight.reshape(down_weight.shape[1:]),
    )
    down, up, pg = pl.pallas_call(
        hand_over,
        out_shape=tuple(jax.ShapeDtypeStruct(a.shape, a.dtype) for a in (down, up, pg)),
        in_specs=[vmem, vmem, vmem],
        out_specs=(vmem, vmem, vmem),
        name="hand_over",
    )(down, up, pg)
    return down[None], up[None], pg.T


def solution(mesh):
    rows = P(("dp", "expert"), None)
    return jax.shard_map(
        per_device,
        mesh=mesh,
        in_specs=(rows, rows, rows, rows, rows, rows, P("expert", None, None)),
        out_specs=(P("expert", "dp", None), P("expert", "dp", None), rows),
        check_vma=False,
    )
```
